32 devices in a mesh: grp: 2 (over y), tm: 4 (over x, core), chan: 4 (over z).
Axes of the slice: x: 2, y: 2, z: 4, core: 2. Of those that a mesh axis runs over, the one named last changes fastest.
Arguments:
- features: bfloat16 [384, 16, 16, 128], P('chan', ('grp', 'tm')), parts along dimension 1, may hold values from -9 to 9, as said below
- gain_in: float32 [384], replicated, may hold values from 0.1 to 1.9
- bias_in: float32 [384], replicated, may hold values from -3 to 3
- weight_in: bfloat16 [3, 3, 3, 384, 384], P(None, None, None, 'chan'), may hold values from -0.1080302 to 0.1080302
- gain_mid: float32 [384], replicated, may hold values from 0.1 to 1.9
- bias_mid: float32 [384], replicated, may hold values from -3 to 3
- weight_mid: bfloat16 [3, 3, 3, 384, 384], P(None, None, None, 'chan'), may hold values from -0.078125 to 0.078125
Outputs:
- decoded: bfloat16 [384, 16, 16, 128], P('chan', ('grp', 'tm')), parts along dimension 1
The draws below stay inside these ranges and needn't reach their ends.
There are 2 independent parts, one for each index of `grp`. The reference program is written for one: setup_inputs(seed, part) draws one part's arguments, and reference() takes and returns one part's arrays. A program takes and returns all parts, laid end to end along the dimension named above; an argument that names none is the same for every part. Nothing has to cross between parts.
Inputs may be any that keep to these rules, and one draw needn't show every extreme that they name: features: channel c has a scale of 0.4 * 3 ** (c / 384 - 0.5) times an independent factor between 0.5 and 2.
All inputs are finite; a program needn't handle non-finite values.
Results may differ from the reference program's by a relative error of at most 0.015.
Values may be sent and summed in bfloat16 or wider, within the bound.
No kernel may reach another device: no remote copies, remote signals or barrier semaphores. Data moves between devices by JAX's collectives and lax.ppermute only.
A program may use at most 64 MiB of HBM per device.

```python
import math
import jax
import jax.numpy as jnp
from jax import lax

C = 384
ROWS = 16
COLS = 128
FRAMES = 8
N_CHAN = 4


def draw_features(key, part):
    base_key = jax.random.fold_in(key, 11)
    rough_key = jax.random.fold_in(key, 12)
    shape = (C, FRAMES, ROWS, COLS)
    ramp = jnp.exp(math.log(3.0) * (jnp.arange(C, dtype=jnp.float32) / C - 0.5))
    rough = jnp.exp(jax.random.uniform(rough_key, (C,), jnp.float32, math.log(0.5), math.log(2.0)))
    channel_scale = (0.4 * ramp * rough)[:, None, None, None]
    base = jnp.clip(jax.random.normal(base_key, shape, jnp.float32), -6.0, 6.0)
    return (base * channel_scale).astype(jnp.bfloat16)


def draw_weight_in(key, part):
    base_key = jax.random.fold_in(key, 21)
    base = jnp.clip(jax.random.normal(base_key, (3, 3, 3, C, C), jnp.float32), -6.0, 6.0)
    ramp = jnp.exp(math.log(3.0) * (jnp.arange(C, dtype=jnp.float32) / C - 0.5))
    return (base * ramp * (27.0 * C) ** (-0.5)).astype(jnp.bfloat16)


def with_spikes(values, own_key, source, target, blocks, factor):
    def block_of(dim):
        return (jnp.arange(values.shape[dim]) // (values.shape[dim] // blocks)).reshape((-1,) + (1,) * (values.ndim - 1 - dim))

    near = jax.random.permutation(own_key, blocks)[block_of(target)]
    far = (block_of(target) + blocks // 2) % blocks
    return jnp.where((block_of(source) == near) | (block_of(source) == far), factor * values, values)


def levels(stream_key, dims, cuts, low, high):
    def one(position, blocks):
        draws = jax.random.uniform(jax.random.fold_in(jax.random.fold_in(stream_key, 6), position), (blocks,), jnp.float32, low / len(cuts), high / len(cuts))
        return jnp.repeat(jnp.exp(draws), dims[position] // blocks).reshape((-1,) + (1,) * (len(dims) - position - 1))

    factor_of = one(*cuts[0])
    for cut in cuts[1:]:
        factor_of = factor_of * one(*cut)
    return factor_of


def scatter_about(rng, extent, spread, reach, shards=(), kind=jnp.bfloat16):
    drawn = jax.random.normal(rng, extent, jnp.float32) * spread
    if len(shards) > 0:
        drawn = levels(rng, extent, shards, -0.22, 0.18) * drawn
    return jnp.clip(drawn, min=-reach, max=reach).astype(kind)


def heavy_noise(stream_key, extent, spread, reach, shards, heavy, held_as=jnp.bfloat16):
    drawn = spread * jax.random.normal(stream_key, extent, jnp.float32)
    if shards:
        drawn = drawn * levels(stream_key, extent, shards, -0.22, 0.18)
    return jnp.clip(with_spikes(drawn, jax.random.fold_in(stream_key, 3), *heavy), -reach, reach).astype(held_as)


def setup_inputs(seed: int = 0, part: int = 0) -> dict:
    key_of = jax.random.split(jax.random.key(seed), 8)
    part_splits = jax.random.split(jax.random.fold_in(key_of[7], part), 8)
    features = draw_features(jax.random.fold_in(jax.random.fold_in(key_of[7], part), 71), part)
    gain_in = jnp.clip(1.0 + 0.18 * jax.random.normal(key_of[1], (C,), jnp.float32), 0.1, 1.9)
    bias_in = scatter_about(key_of[2], (C,), 0.5, 3.0, (), jnp.float32)
    weight_in = draw_weight_in(jax.random.fold_in(key_of[7], 71), part)
    gain_mid = jnp.clip(1.0 + 0.18 * jax.random.normal(key_of[4], (C,), jnp.float32), 0.1, 1.9)
    bias_mid = scatter_about(key_of[5], (C,), 0.5, 3.0, (), jnp.float32)
    weight_mid = heavy_noise(key_of[6], (3, 3, 3, C, C), (27 * C) ** -0.5, 0.078125, ((3, 4),), (3, 4, 4, 2.0))
    return {"features": features, "gain_in": gain_in, "bias_in": bias_in, "weight_in": weight_in, "gain_mid": gain_mid, "bias_mid": bias_mid, "weight_mid": weight_mid}


NORM_EPS = 1e-06

def activate(values, gain):
    values_f32 = values.astype(jnp.float32)
    mean_sq = lax.optimization_barrier(jnp.mean(values_f32 * values_f32, axis=0))
    scaled = values_f32 * lax.rsqrt(mean_sq + NORM_EPS)[None] * gain[:, None, None, None]
    return jax.nn.silu(scaled).astype(jnp.bfloat16)

def causal_conv(activated, weight):
    group_width = C // N_CHAN
    running = jnp.zeros((C, FRAMES, ROWS, COLS), jnp.float32)
    for group_index in range(N_CHAN):
        lower = group_index * group_width
        result = lax.conv_general_dilated(activated[None, lower:lower + group_width], weight[:, :, :, lower:lower + group_width, :], (1, 1, 1), ((2, 0), (1, 1), (1, 1)), dimension_numbers=('NCDHW', 'DHWIO', 'NCDHW'), preferred_element_type=jnp.float32)[0]
        running = running + lax.optimization_barrier(result.astype(jnp.bfloat16)).astype(jnp.float32)
    return running

def reference(features, gain_in, bias_in, weight_in, gain_mid, bias_mid, weight_mid):
    first = activate(features, gain_in)
    hidden = (causal_conv(first, weight_in) + bias_in[:, None, None, None]).astype(jnp.bfloat16)
    second = activate(hidden, gain_mid)
    total = features.astype(jnp.float32) + causal_conv(second, weight_mid) + bias_mid[:, None, None, None]
    return total.astype(jnp.bfloat16)
```

```python
import functools
import jax
import jax.numpy as jnp
from jax import lax
from jax.experimental import pallas as pl
from jax.experimental.pallas import tpu as pltpu
from jax.sharding import PartitionSpec as P

NORM_EPS = 1e-06
BF, F32 = jnp.bfloat16, jnp.float32
VMEM_LIMIT = 60 * 1024 * 1024


def vmem():
    return pl.BlockSpec(memory_space=pltpu.VMEM)


def params():
    return pltpu.CompilerParams(vmem_limit_bytes=VMEM_LIMIT)


def lay_kernel(x_ref, flat_ref, sq_ref, scr):
    chans, frames, rows, cols = x_ref.shape
    for f in range(frames):
        v = x_ref[:, f].astype(F32)
        sq = jnp.sum(v * v, axis=0)
        scr[...] = v.reshape(chans * rows, cols)
        for r in range(rows):
            lanes = slice((f * rows + r) * cols, (f * rows + r + 1) * cols)
            sq_ref[:, lanes] = sq[r : r + 1]
            flat_ref[:, lanes] = scr[pl.ds(r, chans, stride=rows), :].astype(BF)


def lay(x):
    chans, frames, rows, cols = x.shape
    cells = frames * rows * cols
    return pl.pallas_call(
        lay_kernel,
        out_shape=(
            jax.ShapeDtypeStruct((chans, cells), BF),
            jax.ShapeDtypeStruct((1, cells), F32),
        ),
        in_specs=[vmem()],
        out_specs=(vmem(), vmem()),
        scratch_shapes=[pltpu.VMEM((chans * rows, cols), F32)],
        compiler_params=params(),
        name="lay",
    )(x)


def conv_kernel(total, rows, cols, step_rows, x0, x1, x2, s0, s1, s2, gain_ref, w_ref, out_ref, im):
    chans = gain_ref.shape[0]
    slot = (rows + 2) * cols

    @pl.when(pl.program_id(0) == 0)
    def _():
        lane = lax.broadcasted_iota(jnp.int32, (chans, cols), 1)
        gain = jnp.broadcast_to(gain_ref[...], (chans, cols))
        zero = jnp.zeros((3 * chans, cols), BF)
        for f, (x, s) in enumerate(((x0, s0), (x1, s1), (x2, s2))):
            im[0 : 3 * chans, f * slot + cols : f * slot + 2 * cols] = zero
            im[6 * chans : 9 * chans, f * slot + rows * cols : f * slot + (rows + 1) * cols] = zero

            @pl.loop(0, rows // 4)
            def _(q):
                for j in range(4):
                    r = q * 4 + j
                    at = pl.ds(pl.multiple_of(r * cols, cols), cols)
                    inv = lax.rsqrt(s[:, at] * (1.0 / total) + NORM_EPS)
                    u = x[:, at].astype(F32) * inv * gain
                    a = u / (1.0 + jnp.exp(-u))
                    mid = a.astype(BF)
                    left = jnp.where(lane == 0, 0.0, pltpu.roll(a, 1, 1)).astype(BF)
                    right = jnp.where(lane == cols - 1, 0.0, pltpu.roll(a, cols - 1, 1)).astype(BF)
                    for dr in range(3):
                        to = pl.ds(pl.multiple_of(f * slot + (r + 2 - dr) * cols, cols), cols)
                        for dc, v in enumerate((left, mid, right)):
                            k = (dr * 3 + dc) * chans
                            im[k : k + chans, to] = v

    width = step_rows * cols
    acc = None
    for dt in range(3):
        at = pl.multiple_of(dt * slot + cols + pl.program_id(0) * width, cols)
        part = jnp.dot(w_ref[dt], im[:, pl.ds(at, width)], preferred_element_type=F32)
        acc = part if acc is None else acc + part
    out_ref[...] = acc.astype(BF)


def conv(xs, sqs, gain, w, total, rows, cols):
    chans = xs[0].shape[0]
    outs = w.shape[1]
    step_rows = 4
    whole = lambda a: pl.BlockSpec(a.shape, lambda i: (0,) * a.ndim, pipeline_mode=pl.Buffered(1))
    args = (*xs, *sqs, gain[:, None], w)
    return pl.pallas_call(
        functools.partial(conv_kernel, total, rows, cols, step_rows),
        out_shape=jax.ShapeDtypeStruct((outs, rows * cols), BF),
        grid=(rows // step_rows,),
        in_specs=[whole(a) for a in args],
        out_specs=pl.BlockSpec((outs, step_rows * cols), lambda i: (0, i)),
        scratch_shapes=[pltpu.VMEM((9 * chans, 3 * (rows + 2) * cols), BF)],
        compiler_params=params(),
        cost_estimate=pl.CostEstimate(
            flops=2 * 27 * chans * outs * rows * cols,
            bytes_accessed=w.size * 2 + outs * rows * cols * 2,
            transcendentals=0,
        ),
        name="conv",
    )(*args)


def finish_kernel(nf, *refs):
    parts, (x_ref, bias_ref, out_ref, scr) = refs[: 3 * nf], refs[3 * nf :]
    chans, frames, rows, cols = x_ref.shape
    bias = jnp.broadcast_to(bias_ref[...], (chans, cols))
    for f in range(frames):
        a, b, c = parts[3 * f : 3 * f + 3]
        for r in range(rows):
            at = slice(r * cols, (r + 1) * cols)
            v = a[:, at].astype(F32) + b[:, at].astype(F32) + c[:, at].astype(F32)
            scr[pl.ds(r, chans, stride=rows), :] = v + bias
        v = x_ref[:, f].astype(F32) + scr[...].reshape(chans, rows, cols)
        out_ref[:, f] = v.astype(BF)


def finish(parts, x, bias):
    chans, frames, rows, cols = x.shape
    flat = [p for part in parts for p in part]
    return pl.pallas_call(
        functools.partial(finish_kernel, frames),
        out_shape=jax.ShapeDtypeStruct(x.shape, BF),
        in_specs=[vmem()] * (len(flat) + 2),
        out_specs=vmem(),
        scratch_shapes=[pltpu.VMEM((chans * rows, cols), F32)],
        compiler_params=params(),
        name="finish",
    )(*flat, x, bias[:, None])


def sum_over_chan(v):
    n = lax.axis_size("chan")
    by = 1
    while by < n:
        v = v + lax.ppermute(v, "chan", [(i, i ^ by) for i in range(n)])
        by *= 2
    return v


def behind(v):
    n = lax.axis_size("tm")
    return lax.ppermute(v, "tm", [(i, i + 1) for i in range(n - 1)])


def line_scatter(parts):
    n = lax.axis_size("chan")
    me = lax.axis_index("chan")
    right = left = None
    pick = lambda d: lax.dynamic_index_in_dim(parts, jnp.clip(d, 0, n - 1), 0, False)
    for k in range(1, n):
        send_r, send_l = pick(n - k + me), pick(me - (n - k))
        if right is not None:
            send_r = (send_r.astype(F32) + right.astype(F32)).astype(BF)
            send_l = (send_l.astype(F32) + left.astype(F32)).astype(BF)
        ends = range(min(k, n - 1))
        right = lax.ppermute(send_r, "chan", [(z, z + 1) for z in ends])
        left = lax.ppermute(send_l, "chan", [(n - 1 - z, n - 2 - z) for z in ends])
    return pick(me), right, left


def stage(frames_of, sqs_of, halo, halo_sq, gain, w, total, rows, cols):
    frames = [*halo, *frames_of]
    sqs = [*halo_sq, *sqs_of]
    n = lax.axis_size("chan")
    out = []
    for f in range(len(frames_of)):
        y = conv(frames[f : f + 3], sqs[f : f + 3], gain, w, total, rows, cols)
        out.append(line_scatter(y.reshape(n, y.shape[0] // n, y.shape[1])))
    return out


def per_device(features, gain_in, bias_in, weight_in, gain_mid, bias_mid, weight_mid):
    chans, frames, rows, cols = features.shape
    total = chans * lax.axis_size("chan")
    first_chan = lax.axis_index("chan") * chans
    area = rows * cols

    def own(vector):
        return lax.dynamic_slice_in_dim(vector, first_chan, chans, 0)

    def turned(w):
        return jnp.swapaxes(w.reshape(3, 9 * chans, w.shape[-1]), 1, 2)

    def split(v):
        return [v[:, f * area : (f + 1) * area] for f in range(v.shape[1] // area)]

    flat, sq = lay(features)
    halo = behind(flat[:, (frames - 2) * area :])
    sq = sum_over_chan(sq)
    halo_sq = behind(sq[:, (frames - 2) * area :])
    sums = stage(split(flat), split(sq), split(halo), split(halo_sq), own(gain_in), turned(weight_in), total, rows, cols)

    bias = own(bias_in)[:, None]
    hidden = [
        (a.astype(F32) + b.astype(F32) + c.astype(F32) + bias).astype(BF) for a, b, c in sums
    ]
    sq = sum_over_chan(jnp.concatenate([jnp.sum(h.astype(F32) ** 2, axis=0, keepdims=True) for h in hidden], axis=1))
    halo = [behind(h) for h in hidden[-2:]]
    halo_sq = behind(sq[:, (frames - 2) * area :])
    sums = stage(hidden, split(sq), halo, split(halo_sq), own(gain_mid), turned(weight_mid), total, rows, cols)
    return finish(sums, features, own(bias_mid))


def solution(mesh):
    placed = (
        P("chan", ("grp", "tm"), None, None),
        P(),
        P(),
        P(None, None, None, "chan", None),
        P(),
        P(),
        P(None, None, None, "chan", None),
    )
    return jax.shard_map(
        per_device,
        mesh=mesh,
        in_specs=placed,
        out_specs=P("chan", ("grp", "tm"), None, None),
        check_vma=False,
    )
```

```python
import functools
import jax
import jax.numpy as jnp
from jax import lax
from jax.experimental import pallas as pl
from jax.experimental.pallas import tpu as pltpu
from jax.sharding import PartitionSpec as P

NORM_EPS = 1e-06
BF, F32 = jnp.bfloat16, jnp.float32
VMEM_LIMIT = 60 * 1024 * 1024


def vmem():
    return pl.BlockSpec(memory_space=pltpu.VMEM)


def params():
    return pltpu.CompilerParams(vmem_limit_bytes=VMEM_LIMIT)


def lay_kernel(x_ref, flat_ref, sq_ref, scr):
    chans, frames, rows, cols = x_ref.shape
    for f in range(frames):
        v = x_ref[:, f].astype(F32)
        sq = jnp.sum(v * v, axis=0)
        scr[...] = v.reshape(chans * rows, cols)
        for r in range(rows):
            lanes = slice((f * rows + r) * cols, (f * rows + r + 1) * cols)
            sq_ref[:, lanes] = sq[r : r + 1]
            flat_ref[:, lanes] = scr[pl.ds(r, chans, stride=rows), :].astype(BF)


def lay(x):
    chans, frames, rows, cols = x.shape
    cells = frames * rows * cols
    return pl.pallas_call(
        lay_kernel,
        out_shape=(
            jax.ShapeDtypeStruct((chans, cells), BF),
            jax.ShapeDtypeStruct((1, cells), F32),
        ),
        in_specs=[vmem()],
        out_specs=(vmem(), vmem()),
        scratch_shapes=[pltpu.VMEM((chans * rows, cols), F32)],
        compiler_params=params(),
        name="lay",
    )(x)


def conv_kernel(total, rows, cols, step_rows, x0, x1, x2, s0, s1, s2, gain_ref, w_ref, out_ref, im):
    chans = gain_ref.shape[0]
    slot = (rows + 2) * cols

    @pl.when(pl.program_id(0) == 0)
    def _():
        lane = lax.broadcasted_iota(jnp.int32, (chans, cols), 1)
        gain = jnp.broadcast_to(gain_ref[...], (chans, cols))
        zero = jnp.zeros((3 * chans, cols), BF)
        for f, (x, s) in enumerate(((x0, s0), (x1, s1), (x2, s2))):
            im[0 : 3 * chans, f * slot + cols : f * slot + 2 * cols] = zero
            im[6 * chans : 9 * chans, f * slot + rows * cols : f * slot + (rows + 1) * cols] = zero

            @pl.loop(0, rows // 4)
            def _(q):
                for j in range(4):
                    r = q * 4 + j
                    at = pl.ds(pl.multiple_of(r * cols, cols), cols)
                    inv = lax.rsqrt(s[:, at] * (1.0 / total) + NORM_EPS)
                    u = x[:, at].astype(F32) * inv * gain
                    a = u / (1.0 + jnp.exp(-u))
                    mid = a.astype(BF)
                    left = jnp.where(lane == 0, 0.0, pltpu.roll(a, 1, 1)).astype(BF)
                    right = jnp.where(lane == cols - 1, 0.0, pltpu.roll(a, cols - 1, 1)).astype(BF)
                    for dr in range(3):
                        to = pl.ds(pl.multiple_of(f * slot + (r + 2 - dr) * cols, cols), cols)
                        for dc, v in enumerate((left, mid, right)):
                            k = (dr * 3 + dc) * chans
                            im[k : k + chans, to] = v

    width = step_rows * cols
    acc = None
    for dt in range(3):
        at = pl.multiple_of(dt * slot + cols + pl.program_id(0) * width, cols)
        part = jnp.dot(w_ref[dt], im[:, pl.ds(at, width)], preferred_element_type=F32)
        acc = part if acc is None else acc + part
    out_ref[0] = acc.astype(BF)


def conv(xs, sqs, gain, w, total, rows, cols, blocks):
    chans = xs[0].shape[0]
    outs = w.shape[1]
    step_rows = rows // blocks
    whole = lambda a: pl.BlockSpec(a.shape, lambda i: (0,) * a.ndim, pipeline_mode=pl.Buffered(1))
    args = (*xs, *sqs, gain[:, None], w)
    return pl.pallas_call(
        functools.partial(conv_kernel, total, rows, cols, step_rows),
        out_shape=jax.ShapeDtypeStruct((blocks, outs, step_rows * cols), BF),
        grid=(blocks,),
        in_specs=[whole(a) for a in args],
        out_specs=pl.BlockSpec((1, outs, step_rows * cols), lambda i: (i, 0, 0)),
        scratch_shapes=[pltpu.VMEM((9 * chans, 3 * (rows + 2) * cols), BF)],
        compiler_params=params(),
        cost_estimate=pl.CostEstimate(
            flops=2 * 27 * chans * outs * rows * cols,
            bytes_accessed=w.size * 2 + outs * rows * cols * 2,
            transcendentals=0,
        ),
        name="conv",
    )(*args)


def rows_kernel(frames, own_rows, cols, chans, own, up, down, old, old_up, old_down, gain_ref, w_ref, out_ref, im, acc):
    total = gain_ref.shape[0]
    groups = total // chans
    depth = 27 * chans
    width = own_rows * cols

    @pl.when(pl.program_id(0) == 0)
    def _():
        lane = lax.broadcasted_iota(jnp.int32, (chans, cols), 1)
        for fe in range(frames + 2):
            if fe < 2:
                body, above, below, f = old, old_up, old_down, fe
            else:
                body, above, below, f = own, up, down, fe - 2
            for re in range(own_rows + 2):
                if re == 0:
                    src, at = above, slice(f * cols, (f + 1) * cols)
                elif re == own_rows + 1:
                    src, at = below, slice(f * cols, (f + 1) * cols)
                else:
                    src, at = body, slice(f * width + (re - 1) * cols, f * width + re * cols)
                v = src[:, at].astype(F32)
                inv = lax.rsqrt(jnp.sum(v * v, axis=0, keepdims=True) * (1.0 / total) + NORM_EPS)

                @pl.loop(0, groups)
                def _(d):
                    part = pl.ds(pl.multiple_of(d * chans, 8), chans)
                    u = src[part, at].astype(F32) * inv * gain_ref[part, :]
                    a = u / (1.0 + jnp.exp(-u))
                    mid = a.astype(BF)
                    left = jnp.where(lane == 0, 0.0, pltpu.roll(a, 1, 1)).astype(BF)
                    right = jnp.where(lane == cols - 1, 0.0, pltpu.roll(a, cols - 1, 1)).astype(BF)
                    for dt in range(3):
                        t = fe - dt
                        if not 0 <= t < frames:
                            continue
                        for dr in range(3):
                            r = re - dr
                            if not 0 <= r < own_rows:
                                continue
                            to = slice((t * own_rows + r) * cols, (t * own_rows + r + 1) * cols)
                            for dc, x in enumerate((left, mid, right)):
                                k = d * depth + (dt * 9 + dr * 3 + dc) * chans
                                im[pl.ds(pl.multiple_of(k, 8), chans), to] = x

    d = pl.program_id(0)
    at = pl.ds(pl.multiple_of(d * depth, 8), depth)
    for t in range(frames):
        cells = slice(t * width, (t + 1) * width)
        part = jnp.dot(w_ref[0], im[at, cells], preferred_element_type=F32)

        @pl.when(d == 0)
        def _():
            acc[:, cells] = part

        @pl.when(d > 0)
        def _():
            acc[:, cells] += part

    @pl.when(d == groups - 1)
    def _():
        out_ref[...] = acc[...].astype(BF)


def conv_rows(pieces, gain, w, frames, own_rows, cols):
    groups, outs, depth = w.shape
    chans = depth // 27
    whole = lambda a: pl.BlockSpec(a.shape, lambda i: (0,) * a.ndim, pipeline_mode=pl.Buffered(1))
    args = (*pieces, gain[:, None])
    cells = frames * own_rows * cols
    return pl.pallas_call(
        functools.partial(rows_kernel, frames, own_rows, cols, chans),
        out_shape=jax.ShapeDtypeStruct((outs, cells), BF),
        grid=(groups,),
        in_specs=[whole(a) for a in args] + [pl.BlockSpec((1, outs, depth), lambda i: (i, 0, 0))],
        out_specs=pl.BlockSpec((outs, cells), lambda i: (0, 0)),
        scratch_shapes=[pltpu.VMEM((groups * depth, cells), BF), pltpu.VMEM((outs, cells), F32)],
        compiler_params=params(),
        cost_estimate=pl.CostEstimate(
            flops=2 * groups * depth * outs * cells, bytes_accessed=w.size * 2, transcendentals=0
        ),
        name="conv_rows",
    )(*args, w)


def finish_kernel(count, me_ref, *refs):
    parts, (x_ref, bias_ref, out_ref, scr) = refs[:count], refs[count:]
    chans, frames, rows, cols = x_ref.shape
    own_rows = rows // count
    bias = jnp.broadcast_to(bias_ref[...], (chans, cols))
    for f in range(frames):
        for s in range(count):
            first = (me_ref[0] ^ s) * own_rows
            for r in range(own_rows):
                at = slice((f * own_rows + r) * cols, (f * own_rows + r + 1) * cols)
                scr[pl.ds(first + r, chans, stride=rows), :] = parts[s][:, at].astype(F32) + bias
        v = x_ref[:, f].astype(F32) + scr[...].reshape(chans, rows, cols)
        out_ref[:, f] = v.astype(BF)


def finish(parts, x, bias, me):
    chans, frames, rows, cols = x.shape
    return pl.pallas_call(
        functools.partial(finish_kernel, len(parts)),
        out_shape=jax.ShapeDtypeStruct(x.shape, BF),
        in_specs=[pl.BlockSpec(memory_space=pltpu.SMEM)] + [vmem()] * (len(parts) + 2),
        out_specs=vmem(),
        scratch_shapes=[pltpu.VMEM((chans * rows, cols), F32)],
        compiler_params=params(),
        name="finish",
    )(me[None], *parts, x, bias[:, None])


def sum_over_chan(v):
    n = lax.axis_size("chan")
    by = 1
    while by < n:
        v = v + lax.ppermute(v, "chan", [(i, i ^ by) for i in range(n)])
        by *= 2
    return v


def behind(v):
    n = lax.axis_size("tm")
    return lax.ppermute(v, "tm", [(i, i + 1) for i in range(n - 1)])


def line_scatter(parts):
    n = lax.axis_size("chan")
    me = lax.axis_index("chan")
    right = left = None
    pick = lambda d: lax.dynamic_index_in_dim(parts, jnp.clip(d, 0, n - 1), 0, False)
    for k in range(1, n):
        send_r, send_l = pick(n - k + me), pick(me - (n - k))
        if right is not None:
            send_r = (send_r.astype(F32) + right.astype(F32)).astype(BF)
            send_l = (send_l.astype(F32) + left.astype(F32)).astype(BF)
        ends = range(min(k, n - 1))
        right = lax.ppermute(send_r, "chan", [(z, z + 1) for z in ends])
        left = lax.ppermute(send_l, "chan", [(n - 1 - z, n - 2 - z) for z in ends])
    return pick(me), right, left


def shifted(v, frames_by, rows_by):
    tm, n = lax.axis_size("tm"), lax.axis_size("chan")
    pairs = [
        (t * n + z + rows_by, (t + frames_by) * n + z)
        for t in range(tm - frames_by)
        for z in range(n)
        if 0 <= z + rows_by < n
    ]
    return lax.ppermute(v, ("tm", "chan"), pairs)


def per_device(features, gain_in, bias_in, weight_in, gain_mid, bias_mid, weight_mid):
    chans, frames, rows, cols = features.shape
    n = lax.axis_size("chan")
    me = lax.axis_index("chan")
    total = chans * n
    area = rows * cols
    own_rows = rows // n
    width = own_rows * cols

    def own(vector):
        return lax.dynamic_slice_in_dim(vector, me * chans, chans, 0)

    def split(v):
        return [v[:, f * area : (f + 1) * area] for f in range(v.shape[1] // area)]

    peers = lax.axis_size("grp") * lax.axis_size("tm")
    share = total // peers
    rank = lax.axis_index("grp") * lax.axis_size("tm") + lax.axis_index("tm")
    piece = lax.dynamic_slice_in_dim(weight_mid.reshape(27 * chans, total), rank * share, share, 1)
    gathered = lax.all_gather(piece.T, ("chan", "grp", "tm"), axis=0, tiled=False)
    w_mid = gathered.reshape(n, total, 27 * chans)
    w_in = jnp.swapaxes(weight_in.reshape(3, 9 * chans, total), 1, 2)

    flat, sq = lay(features)
    halo = behind(flat[:, (frames - 2) * area :])
    sq = sum_over_chan(sq)
    halo_sq = behind(sq[:, (frames - 2) * area :])
    xs = [*split(halo), *split(flat)]
    sqs = [*split(halo_sq), *split(sq)]
    sums = []
    for f in range(frames):
        y = conv(xs[f : f + 3], sqs[f : f + 3], own(gain_in), w_in, total, rows, cols, n)
        sums.append(line_scatter(y))

    bias = bias_in[:, None]
    hidden = jnp.concatenate(
        [(a.astype(F32) + b.astype(F32) + c.astype(F32) + bias).astype(BF) for a, b, c in sums],
        axis=1,
    )
    cube = hidden.reshape(total, frames, width)
    top = cube[:, :, :cols].reshape(total, frames * cols)
    bottom = cube[:, :, width - cols :].reshape(total, frames * cols)
    pieces = (
        hidden,
        shifted(bottom, 0, -1),
        shifted(top, 0, 1),
        shifted(hidden[:, (frames - 2) * width :], 1, 0),
        shifted(bottom[:, (frames - 2) * cols :], 1, -1),
        shifted(top[:, (frames - 2) * cols :], 1, 1),
    )
    y = conv_rows(pieces, gain_mid, w_mid, frames, own_rows, cols)
    y = y.reshape(n, chans, frames * width)
    parts = []
    for s in range(n):
        part = lax.dynamic_index_in_dim(y, me ^ s, 0, False)
        parts.append(part if s == 0 else lax.ppermute(part, "chan", [(i, i ^ s) for i in range(n)]))
    return finish(parts, features, own(bias_mid), me)


def solution(mesh):
    placed = (
        P("chan", ("grp", "tm"), None, None),
        P(),
        P(),
        P(None, None, None, "chan", None),
        P(),
        P(),
        P(None, None, None, "chan", None),
    )
    return jax.shard_map(
        per_device,
        mesh=mesh,
        in_specs=placed,
        out_specs=P("chan", ("grp", "tm"), None, None),
        check_vma=False,
    )
```

```python
import functools
import jax
import jax.numpy as jnp
from jax import lax
from jax.experimental import pallas as pl
from jax.experimental.pallas import tpu as pltpu
from jax.sharding import PartitionSpec as P

NORM_EPS = 1e-06
BF, F32 = jnp.bfloat16, jnp.float32
MIB = 1024 * 1024


def vmem():
    return pl.BlockSpec(memory_space=pltpu.VMEM)


def params(mib):
    return pltpu.CompilerParams(vmem_limit_bytes=mib * MIB)


def lay_kernel(x_ref, flat_ref, sq_ref, scr):
    chans, frames, rows, cols = x_ref.shape
    for f in range(frames):
        v = x_ref[:, f].astype(F32)
        sq = jnp.sum(v * v, axis=0)
        scr[...] = v.reshape(chans * rows, cols)
        for r in range(rows):
            lanes = slice((f * rows + r) * cols, (f * rows + r + 1) * cols)
            sq_ref[:, lanes] = sq[r : r + 1]
            flat_ref[:, lanes] = scr[pl.ds(r, chans, stride=rows), :].astype(BF)


def lay(x):
    chans, frames, rows, cols = x.shape
    cells = frames * rows * cols
    return pl.pallas_call(
        lay_kernel,
        out_shape=(
            jax.ShapeDtypeStruct((chans, cells), BF),
            jax.ShapeDtypeStruct((1, cells), F32),
        ),
        in_specs=[vmem()],
        out_specs=(vmem(), vmem()),
        scratch_shapes=[pltpu.VMEM((chans * rows, cols), F32)],
        compiler_params=params(8),
        name="lay",
    )(x)


def conv_kernel(total, rows, cols, step_rows, x0, x1, x2, s0, s1, s2, gain_ref, w_ref, out_ref, im):
    chans = gain_ref.shape[0]
    slot = (rows + 2) * cols

    @pl.when(pl.program_id(0) == 0)
    def _():
        lane = lax.broadcasted_iota(jnp.int32, (chans, cols), 1)
        gain = jnp.broadcast_to(gain_ref[...], (chans, cols))
        zero = jnp.zeros((3 * chans, cols), BF)
        for f, (x, s) in enumerate(((x0, s0), (x1, s1), (x2, s2))):
            im[0 : 3 * chans, f * slot + cols : f * slot + 2 * cols] = zero
            im[6 * chans : 9 * chans, f * slot + rows * cols : f * slot + (rows + 1) * cols] = zero

            @pl.loop(0, rows // 4)
            def _(q):
                for j in range(4):
                    r = q * 4 + j
                    at = pl.ds(pl.multiple_of(r * cols, cols), cols)
                    inv = lax.rsqrt(s[:, at] * (1.0 / total) + NORM_EPS)
                    u = x[:, at].astype(F32) * inv * gain
                    a = u / (1.0 + jnp.exp(-u))
                    mid = a.astype(BF)
                    left = jnp.where(lane == 0, 0.0, pltpu.roll(a, 1, 1)).astype(BF)
                    right = jnp.where(lane == cols - 1, 0.0, pltpu.roll(a, cols - 1, 1)).astype(BF)
                    for dr in range(3):
                        to = pl.ds(pl.multiple_of(f * slot + (r + 2 - dr) * cols, cols), cols)
                        for dc, v in enumerate((left, mid, right)):
                            k = (dr * 3 + dc) * chans
                            im[k : k + chans, to] = v

    width = step_rows * cols
    acc = None
    for dt in range(3):
        at = pl.multiple_of(dt * slot + cols + pl.program_id(0) * width, cols)
        part = jnp.dot(w_ref[dt], im[:, pl.ds(at, width)], preferred_element_type=F32)
        acc = part if acc is None else acc + part
    out_ref[0] = acc.astype(BF)


def conv(xs, sqs, gain, w, total, rows, cols, blocks):
    chans = xs[0].shape[0]
    outs = w.shape[1]
    step_rows = rows // blocks
    whole = lambda a: pl.BlockSpec(a.shape, lambda i: (0,) * a.ndim, pipeline_mode=pl.Buffered(1))
    args = (*xs, *sqs, gain[:, None], w)
    return pl.pallas_call(
        functools.partial(conv_kernel, total, rows, cols, step_rows),
        out_shape=jax.ShapeDtypeStruct((blocks, outs, step_rows * cols), BF),
        grid=(blocks,),
        in_specs=[whole(a) for a in args],
        out_specs=pl.BlockSpec((1, outs, step_rows * cols), lambda i: (i, 0, 0)),
        scratch_shapes=[pltpu.VMEM((9 * chans, 3 * (rows + 2) * cols), BF)],
        compiler_params=params(22),
        cost_estimate=pl.CostEstimate(
            flops=2 * 27 * chans * outs * rows * cols,
            bytes_accessed=w.size * 2 + outs * rows * cols * 2,
            transcendentals=0,
        ),
        name="conv",
    )(*args)


def rows_kernel(frames, own_rows, cols, chans, own, up, down, old, old_up, old_down, gain_ref, w_ref, out_ref, im, acc):
    total = gain_ref.shape[0]
    groups = total // chans
    depth = 27 * chans
    width = own_rows * cols
    tile = 16 if chans % 16 == 0 else 8

    @pl.when(pl.program_id(0) == 0)
    def _():
        lane = lax.broadcasted_iota(jnp.int32, (chans, cols), 1)
        for fe in range(frames + 2):
            if fe < 2:
                body, above, below, f = old, old_up, old_down, fe
            else:
                body, above, below, f = own, up, down, fe - 2
            for re in range(own_rows + 2):
                if re == 0:
                    src, at = above, slice(f * cols, (f + 1) * cols)
                elif re == own_rows + 1:
                    src, at = below, slice(f * cols, (f + 1) * cols)
                else:
                    src, at = body, slice(f * width + (re - 1) * cols, f * width + re * cols)
                v = src[:, at].astype(F32)
                inv = lax.rsqrt(jnp.sum(v * v, axis=0, keepdims=True) * (1.0 / total) + NORM_EPS)

                @pl.loop(0, groups, unroll=min(groups, 4))
                def _(d):
                    part = pl.ds(pl.multiple_of(d * chans, tile), chans)
                    u = src[part, at].astype(F32) * inv * gain_ref[part, :]
                    a = u / (1.0 + jnp.exp(-u))
                    mid = a.astype(BF)
                    left = jnp.where(lane == 0, 0.0, pltpu.roll(a, 1, 1)).astype(BF)
                    right = jnp.where(lane == cols - 1, 0.0, pltpu.roll(a, cols - 1, 1)).astype(BF)
                    for dt in range(3):
                        t = fe - dt
                        if not 0 <= t < frames:
                            continue
                        for dr in range(3):
                            r = re - dr
                            if not 0 <= r < own_rows:
                                continue
                            to = slice((t * own_rows + r) * cols, (t * own_rows + r + 1) * cols)
                            for dc, x in enumerate((left, mid, right)):
                                k = d * depth + (dt * 9 + dr * 3 + dc) * chans
                                im[pl.ds(pl.multiple_of(k, tile), chans), to] = x

    d = pl.program_id(0)
    at = pl.ds(pl.multiple_of(d * depth, tile), depth)
    for t in range(frames):
        cells = slice(t * width, (t + 1) * width)
        part = jnp.dot(w_ref[...].reshape(total, depth), im[at, cells], preferred_element_type=F32)

        @pl.when(d == 0)
        def _():
            acc[:, cells] = part

        @pl.when(d > 0)
        def _():
            acc[:, cells] += part

    @pl.when(d == groups - 1)
    def _():
        out_ref[...] = acc[...].astype(BF)


def conv_rows(pieces, gain, w, frames, own_rows, cols):
    shares, groups, share, depth = w.shape
    outs = shares * share
    chans = depth // 27
    whole = lambda a: pl.BlockSpec(a.shape, lambda i: (0,) * a.ndim, pipeline_mode=pl.Buffered(1))
    args = (*pieces, gain[:, None])
    cells = frames * own_rows * cols
    return pl.pallas_call(
        functools.partial(rows_kernel, frames, own_rows, cols, chans),
        out_shape=jax.ShapeDtypeStruct((outs, cells), BF),
        grid=(groups,),
        in_specs=[whole(a) for a in args] + [pl.BlockSpec((shares, 1, share, depth), lambda i: (0, i, 0, 0))],
        out_specs=pl.BlockSpec((outs, cells), lambda i: (0, 0)),
        scratch_shapes=[pltpu.VMEM((groups * depth, cells), BF), pltpu.VMEM((outs, cells), F32)],
        compiler_params=params(36),
        cost_estimate=pl.CostEstimate(
            flops=2 * groups * depth * outs * cells, bytes_accessed=w.size * 2, transcendentals=0
        ),
        name="conv_rows",
    )(*args, w)


def finish_kernel(count, me_ref, *refs):
    parts, (x_ref, bias_ref, out_ref, scr) = refs[:count], refs[count:]
    chans, frames, rows, cols = x_ref.shape
    own_rows = rows // count
    bias = jnp.broadcast_to(bias_ref[...], (chans, cols))
    for f in range(frames):
        for s in range(count):
            first = (me_ref[0] ^ s) * own_rows
            for r in range(own_rows):
                at = slice((f * own_rows + r) * cols, (f * own_rows + r + 1) * cols)
                scr[pl.ds(first + r, chans, stride=rows), :] = parts[s][:, at].astype(F32) + bias
        v = x_ref[:, f].astype(F32) + scr[...].reshape(chans, rows, cols)
        out_ref[:, f] = v.astype(BF)


def finish(parts, x, bias, me):
    chans, frames, rows, cols = x.shape
    return pl.pallas_call(
        functools.partial(finish_kernel, len(parts)),
        out_shape=jax.ShapeDtypeStruct(x.shape, BF),
        in_specs=[pl.BlockSpec(memory_space=pltpu.SMEM)] + [vmem()] * (len(parts) + 2),
        out_specs=vmem(),
        scratch_shapes=[pltpu.VMEM((chans * rows, cols), F32)],
        compiler_params=params(8),
        name="finish",
    )(me[None], *parts, x, bias[:, None])


def sum_over_chan(v):
    n = lax.axis_size("chan")
    by = 1
    while by < n:
        v = v + lax.ppermute(v, "chan", [(i, i ^ by) for i in range(n)])
        by *= 2
    return v


def behind(v):
    n = lax.axis_size("tm")
    return lax.ppermute(v, "tm", [(i, i + 1) for i in range(n - 1)])


def line_scatter(parts):
    n = lax.axis_size("chan")
    me = lax.axis_index("chan")
    pick = lambda d: lax.dynamic_index_in_dim(parts, jnp.clip(d, 0, n - 1), 0, False)
    right = left = None
    for k in range(1, n):
        if k == 1 and n > 3:
            got = lax.ppermute(pick(jnp.where(me == 0, n - 1, 0)), "chan", [(0, 1), (n - 1, n - 2)])
            zero = jnp.zeros_like(got)
            right, left = jnp.where(me == 1, got, zero), jnp.where(me == n - 2, got, zero)
            continue
        send_r, send_l = pick(n - k + me), pick(me - (n - k))
        if right is not None:
            send_r = (send_r.astype(F32) + right.astype(F32)).astype(BF)
            send_l = (send_l.astype(F32) + left.astype(F32)).astype(BF)
        ends = range(min(k, n - 1))
        right = lax.ppermute(send_r, "chan", [(z, z + 1) for z in ends])
        left = lax.ppermute(send_l, "chan", [(n - 1 - z, n - 2 - z) for z in ends])
    return pick(me), right, left


def shifted(v, frames_by, rows_by):
    tm, n = lax.axis_size("tm"), lax.axis_size("chan")
    pairs = [
        (t * n + z + rows_by, (t + frames_by) * n + z)
        for t in range(tm - frames_by)
        for z in range(n)
        if 0 <= z + rows_by < n
    ]
    return lax.ppermute(v, ("tm", "chan"), pairs)


def per_device(features, gain_in, bias_in, weight_in, gain_mid, bias_mid, weight_mid):
    chans, frames, rows, cols = features.shape
    n = lax.axis_size("chan")
    me = lax.axis_index("chan")
    total = chans * n
    area = rows * cols
    own_rows = rows // n
    width = own_rows * cols

    def own(vector):
        return lax.dynamic_slice_in_dim(vector, me * chans, chans, 0)

    def split(v):
        return [v[:, f * area : (f + 1) * area] for f in range(v.shape[1] // area)]

    peers = lax.axis_size("grp") * lax.axis_size("tm")
    share = total // peers
    rank = lax.axis_index("grp") * lax.axis_size("tm") + lax.axis_index("tm")
    piece = lax.dynamic_slice_in_dim(weight_mid.reshape(27 * chans, total), rank * share, share, 1)
    gathered = lax.all_gather(jnp.pad(piece.T, ((0, 8), (0, 0))), "chan", axis=0, tiled=False)
    w_in = jnp.swapaxes(weight_in.reshape(3, 9 * chans, total), 1, 2)

    flat, sq = lay(features)
    halo = behind(flat[:, (frames - 2) * area :])
    sq = sum_over_chan(sq)
    halo_sq = behind(sq[:, (frames - 2) * area :])
    xs = [*split(halo), *split(flat)]
    sqs = [*split(halo_sq), *split(sq)]
    sums = []
    for f in range(frames):
        y = conv(xs[f : f + 3], sqs[f : f + 3], own(gain_in), w_in, total, rows, cols, n)
        if f == frames - 1:
            gathered, y = lax.optimization_barrier((gathered, y))
            w_mid = lax.all_gather(gathered[:, :share], ("grp", "tm"), axis=0, tiled=False)
        sums.append(line_scatter(y))

    bias = bias_in[:, None]
    hidden = jnp.concatenate(
        [(a.astype(F32) + b.astype(F32) + c.astype(F32) + bias).astype(BF) for a, b, c in sums],
        axis=1,
    )
    cube = hidden.reshape(total, frames, width)
    top = cube[:, :, :cols].reshape(total, frames * cols)
    bottom = cube[:, :, width - cols :].reshape(total, frames * cols)
    pieces = (
        hidden,
        shifted(bottom, 0, -1),
        shifted(top, 0, 1),
        shifted(hidden[:, (frames - 2) * width :], 1, 0),
        shifted(bottom[:, (frames - 2) * cols :], 1, -1),
        shifted(top[:, (frames - 2) * cols :], 1, 1),
    )
    y = conv_rows(pieces, gain_mid, w_mid, frames, own_rows, cols)
    y = y.reshape(n, chans, frames * width)
    parts = []
    for s in range(n):
        part = lax.dynamic_index_in_dim(y, me ^ s, 0, False)
        parts.append(part if s == 0 else lax.ppermute(part, "chan", [(i, i ^ s) for i in range(n)]))
    return finish(parts, features, own(bias_mid), me)


def solution(mesh):
    placed = (
        P("chan", ("grp", "tm"), None, None),
        P(),
        P(),
        P(None, None, None, "chan", None),
        P(),
        P(),
        P(None, None, None, "chan", None),
    )
    return jax.shard_map(
        per_device,
        mesh=mesh,
        in_specs=placed,
        out_specs=P("chan", ("grp", "tm"), None, None),
        check_vma=False,
    )
```

```python
import functools
import jax
import jax.numpy as jnp
from jax import lax
from jax.experimental import pallas as pl
from jax.experimental.pallas import tpu as pltpu
from jax.sharding import PartitionSpec as P

NORM_EPS = 1e-06
BF, F32 = jnp.bfloat16, jnp.float32
MIB = 1024 * 1024
PER_CALL = 2


def vmem():
    return pl.BlockSpec(memory_space=pltpu.VMEM)


def params(mib):
    return pltpu.CompilerParams(vmem_limit_bytes=mib * MIB)


def lay_kernel(x_ref, flat_ref, sq_ref, scr):
    chans, frames, rows, cols = x_ref.shape
    for f in range(frames):
        v = x_ref[:, f].astype(F32)
        sq = jnp.sum(v * v, axis=0)
        scr[...] = v.reshape(chans * rows, cols)
        for r in range(rows):
            lanes = slice((f * rows + r) * cols, (f * rows + r + 1) * cols)
            sq_ref[:, lanes] = sq[r : r + 1]
            flat_ref[:, lanes] = scr[pl.ds(r, chans, stride=rows), :].astype(BF)


def lay(x):
    chans, frames, rows, cols = x.shape
    cells = frames * rows * cols
    return pl.pallas_call(
        lay_kernel,
        out_shape=(
            jax.ShapeDtypeStruct((chans, cells), BF),
            jax.ShapeDtypeStruct((1, cells), F32),
        ),
        in_specs=[vmem()],
        out_specs=(vmem(), vmem()),
        scratch_shapes=[pltpu.VMEM((chans * rows, cols), F32)],
        compiler_params=params(8),
        name="lay",
    )(x)


def conv_kernel(total, rows, cols, step_rows, x0, x1, x2, s0, s1, s2, gain_ref, w_ref, out_ref, im):
    chans = gain_ref.shape[0]
    slot = (rows + 2) * cols

    @pl.when(pl.program_id(0) == 0)
    def _():
        lane = lax.broadcasted_iota(jnp.int32, (chans, cols), 1)
        gain = jnp.broadcast_to(gain_ref[...], (chans, cols))
        zero = jnp.zeros((3 * chans, cols), BF)
        for f, (x, s) in enumerate(((x0, s0), (x1, s1), (x2, s2))):
            im[0 : 3 * chans, f * slot + cols : f * slot + 2 * cols] = zero
            im[6 * chans : 9 * chans, f * slot + rows * cols : f * slot + (rows + 1) * cols] = zero

            @pl.loop(0, rows // 4)
            def _(q):
                for j in range(4):
                    r = q * 4 + j
                    at = pl.ds(pl.multiple_of(r * cols, cols), cols)
                    inv = lax.rsqrt(s[:, at] * (1.0 / total) + NORM_EPS)
                    u = x[:, at].astype(F32) * inv * gain
                    a = u / (1.0 + jnp.exp(-u))
                    mid = a.astype(BF)
                    left = jnp.where(lane == 0, 0.0, pltpu.roll(a, 1, 1)).astype(BF)
                    right = jnp.where(lane == cols - 1, 0.0, pltpu.roll(a, cols - 1, 1)).astype(BF)
                    for dr in range(3):
                        to = pl.ds(pl.multiple_of(f * slot + (r + 2 - dr) * cols, cols), cols)
                        for dc, v in enumerate((left, mid, right)):
                            k = (dr * 3 + dc) * chans
                            im[k : k + chans, to] = v

    width = step_rows * cols
    acc = None
    for dt in range(3):
        at = pl.multiple_of(dt * slot + cols + pl.program_id(0) * width, cols)
        part = jnp.dot(w_ref[dt], im[:, pl.ds(at, width)], preferred_element_type=F32)
        acc = part if acc is None else acc + part
    out_ref[0] = acc.astype(BF)


def conv(xs, sqs, gain, w, total, rows, cols, blocks):
    chans = xs[0].shape[0]
    outs = w.shape[1]
    step_rows = rows // blocks
    whole = lambda a: pl.BlockSpec(a.shape, lambda i: (0,) * a.ndim, pipeline_mode=pl.Buffered(1))
    args = (*xs, *sqs, gain[:, None], w)
    return pl.pallas_call(
        functools.partial(conv_kernel, total, rows, cols, step_rows),
        out_shape=jax.ShapeDtypeStruct((blocks, outs, step_rows * cols), BF),
        grid=(blocks,),
        in_specs=[whole(a) for a in args],
        out_specs=pl.BlockSpec((1, outs, step_rows * cols), lambda i: (i, 0, 0)),
        scratch_shapes=[pltpu.VMEM((9 * chans, 3 * (rows + 2) * cols), BF)],
        compiler_params=params(22),
        cost_estimate=pl.CostEstimate(
            flops=2 * 27 * chans * outs * rows * cols,
            bytes_accessed=w.size * 2 + outs * rows * cols * 2,
            transcendentals=0,
        ),
        name="conv",
    )(*args)


def rows_kernel(frames, first, local, own_rows, cols, chans, up, down, old_up, old_down, *refs):
    bodies, (gain_ref, w_ref, out_ref, im, acc) = refs[: frames + 2], refs[frames + 2 :]
    total = gain_ref.shape[0]
    groups = total // chans
    depth = 27 * chans
    width = own_rows * cols
    tile = 16 if chans % 16 == 0 else 8
    share = total // w_ref.shape[0]

    @pl.when(pl.program_id(0) == 0)
    def _():
        lane = lax.broadcasted_iota(jnp.int32, (chans, cols), 1)
        for fe in range(frames + 2):
            f = first + fe
            above, below, f = (old_up, old_down, f) if f < 2 else (up, down, f - 2)
            for re in range(own_rows + 2):
                if re == 0:
                    src, at = above, slice(f * cols, (f + 1) * cols)
                elif re == own_rows + 1:
                    src, at = below, slice(f * cols, (f + 1) * cols)
                else:
                    src, at = bodies[fe], slice((re - 1) * cols, re * cols)
                v = src[:, at].astype(F32)
                inv = lax.rsqrt(jnp.sum(v * v, axis=0, keepdims=True) * (1.0 / total) + NORM_EPS)

                @pl.loop(0, groups, unroll=min(groups, 4))
                def _(d):
                    part = pl.ds(pl.multiple_of(d * chans, tile), chans)
                    u = src[part, at].astype(F32) * inv * gain_ref[part, :]
                    a = u / (1.0 + jnp.exp(-u))
                    mid = a.astype(BF)
                    left = jnp.where(lane == 0, 0.0, pltpu.roll(a, 1, 1)).astype(BF)
                    right = jnp.where(lane == cols - 1, 0.0, pltpu.roll(a, cols - 1, 1)).astype(BF)
                    for dt in range(3):
                        t = fe - dt
                        if not 0 <= t < frames:
                            continue
                        for dr in range(3):
                            r = re - dr
                            if not 0 <= r < own_rows:
                                continue
                            to = slice((t * own_rows + r) * cols, (t * own_rows + r + 1) * cols)
                            for dc, x in enumerate((left, mid, right)):
                                k = d * depth + (dt * 9 + dr * 3 + dc) * chans
                                im[pl.ds(pl.multiple_of(k, tile), chans), to] = x

    d = pl.program_id(0)
    at = pl.ds(pl.multiple_of(d * depth, tile), depth)
    for t in range(frames):
        cells = slice(t * width, (t + 1) * width)
        part = jnp.dot(w_ref[:, 0, :share].reshape(total, depth), im[at, cells], preferred_element_type=F32)

        @pl.when(d == 0)
        def _():
            acc[:, cells] = part

        @pl.when(d > 0)
        def _():
            acc[:, cells] += part

    @pl.when(d == groups - 1)
    def _():
        out_ref[...] = acc[...].astype(BF)


def conv_rows(edges, bodies, gain, w, first, local, own_rows, cols):
    shares, groups, share, depth = w.shape
    outs = gain.shape[0]
    chans = depth // 27
    whole = lambda a: pl.BlockSpec(a.shape, lambda i: (0,) * a.ndim, pipeline_mode=pl.Buffered(1))
    frames = len(bodies) - 2
    args = (*edges, *bodies, gain[:, None])
    cells = frames * own_rows * cols
    return pl.pallas_call(
        functools.partial(rows_kernel, frames, first, local, own_rows, cols, chans),
        out_shape=jax.ShapeDtypeStruct((outs, cells), BF),
        grid=(groups,),
        in_specs=[whole(a) for a in args] + [pl.BlockSpec((shares, 1, share, depth), lambda i: (0, i, 0, 0))],
        out_specs=pl.BlockSpec((outs, cells), lambda i: (0, 0)),
        scratch_shapes=[pltpu.VMEM((groups * depth, cells), BF), pltpu.VMEM((outs, cells), F32)],
        compiler_params=params(52),
        cost_estimate=pl.CostEstimate(
            flops=2 * groups * depth * outs * cells, bytes_accessed=w.size * 2, transcendentals=0
        ),
        name="conv_rows",
    )(*args, w)


def finish_kernel(count, me_ref, *refs):
    parts, (x_ref, bias_ref, out_ref, scr) = refs[:-4], refs[-4:]
    chans, frames, rows, cols = x_ref.shape
    own_rows = rows // count
    per_call = frames * count // len(parts)
    bias = jnp.broadcast_to(bias_ref[...], (chans, cols))
    for f in range(frames):
        for s in range(count):
            first = (me_ref[0] ^ s) * own_rows
            part = parts[f // per_call * count + s]
            for r in range(own_rows):
                k = f % per_call * own_rows + r
                v = part[:, k * cols : (k + 1) * cols].astype(F32) + bias
                scr[pl.ds(first + r, chans, stride=rows), :] = v
        v = x_ref[:, f].astype(F32) + scr[...].reshape(chans, rows, cols)
        out_ref[:, f] = v.astype(BF)


def finish(outs, x, bias, me):
    chans, frames, rows, cols = x.shape
    parts = [p for out in outs for p in out]
    return pl.pallas_call(
        functools.partial(finish_kernel, len(outs[0])),
        out_shape=jax.ShapeDtypeStruct(x.shape, BF),
        in_specs=[pl.BlockSpec(memory_space=pltpu.SMEM)] + [vmem()] * (len(parts) + 2),
        out_specs=vmem(),
        scratch_shapes=[pltpu.VMEM((chans * rows, cols), F32)],
        compiler_params=params(8),
        name="finish",
    )(me[None], *parts, x, bias[:, None])


def sum_over_chan(v):
    n = lax.axis_size("chan")
    by = 1
    while by < n:
        v = v + lax.ppermute(v, "chan", [(i, i ^ by) for i in range(n)])
        by *= 2
    return v


def behind(v):
    n = lax.axis_size("tm")
    return lax.ppermute(v, "tm", [(i, i + 1) for i in range(n - 1)])


def line_scatter(parts, late=None):
    n = lax.axis_size("chan")
    me = lax.axis_index("chan")
    pick = lambda d: lax.dynamic_index_in_dim(parts, jnp.clip(d, 0, n - 1), 0, False)
    right = left = None
    for k in range(1, n):
        if k == 1 and n > 3:
            got = lax.ppermute(pick(jnp.where(me == 0, n - 1, 0)), "chan", [(0, 1), (n - 1, n - 2)])
            if late is not None:
                got, late = lax.optimization_barrier((got, late))
            zero = jnp.zeros_like(got)
            right, left = jnp.where(me == 1, got, zero), jnp.where(me == n - 2, got, zero)
            continue
        send_r, send_l = pick(n - k + me), pick(me - (n - k))
        if right is not None:
            send_r = (send_r.astype(F32) + right.astype(F32)).astype(BF)
            send_l = (send_l.astype(F32) + left.astype(F32)).astype(BF)
        ends = range(min(k, n - 1))
        right = lax.ppermute(send_r, "chan", [(z, z + 1) for z in ends])
        left = lax.ppermute(send_l, "chan", [(n - 1 - z, n - 2 - z) for z in ends])
    return (pick(me), right, left), late


def shifted(v, frames_by, rows_by):
    tm, n = lax.axis_size("tm"), lax.axis_size("chan")
    pairs = [
        (t * n + z + rows_by, (t + frames_by) * n + z)
        for t in range(tm - frames_by)
        for z in range(n)
        if 0 <= z + rows_by < n
    ]
    return lax.ppermute(v, ("tm", "chan"), pairs)


def per_device(features, gain_in, bias_in, weight_in, gain_mid, bias_mid, weight_mid):
    chans, frames, rows, cols = features.shape
    n = lax.axis_size("chan")
    me = lax.axis_index("chan")
    total = chans * n
    area = rows * cols
    own_rows = rows // n
    width = own_rows * cols

    def own(vector):
        return lax.dynamic_slice_in_dim(vector, me * chans, chans, 0)

    def split(v):
        return [v[:, f * area : (f + 1) * area] for f in range(v.shape[1] // area)]

    peers = lax.axis_size("grp") * lax.axis_size("tm")
    share = total // peers
    rank = lax.axis_index("grp") * lax.axis_size("tm") + lax.axis_index("tm")
    piece = lax.dynamic_slice_in_dim(weight_mid.reshape(27 * chans, total), rank * share, share, 1)
    gathered = lax.all_gather(jnp.pad(piece.T, ((0, 8), (0, 0))), "chan", axis=0, tiled=False)
    w_in = jnp.swapaxes(weight_in.reshape(3, 9 * chans, total), 1, 2)

    flat, sq = lay(features)
    halo = behind(flat[:, (frames - 2) * area :])
    sq = sum_over_chan(sq)
    halo_sq = behind(sq[:, (frames - 2) * area :])
    xs = [*split(halo), *split(flat)]
    sqs = [*split(halo_sq), *split(sq)]
    ys = [
        conv(xs[f : f + 3], sqs[f : f + 3], own(gain_in), w_in, total, rows, cols, n)
        for f in range(frames)
    ]
    added, (gathered, *ys[1:]) = line_scatter(ys[0], (gathered, *ys[1:]))
    sums = [added, *(line_scatter(y)[0] for y in ys[1:])]
    w_mid = lax.all_gather(gathered, ("grp", "tm"), axis=0, tiled=False)

    bias = bias_in[:, None]
    hidden = [(a.astype(F32) + b.astype(F32) + c.astype(F32) + bias).astype(BF) for a, b, c in sums]
    old = [shifted(h, 1, 0) for h in hidden[-2:]]
    top = jnp.concatenate([h[:, :cols] for h in hidden], axis=1)
    bottom = jnp.concatenate([h[:, width - cols :] for h in hidden], axis=1)
    last = slice((frames - 2) * cols, None)
    edges = (
        shifted(bottom, 0, -1),
        shifted(top, 0, 1),
        shifted(bottom[:, last], 1, -1),
        shifted(top[:, last], 1, 1),
    )
    bodies = [*old, *hidden]
    outs = []
    for f in range(0, frames, PER_CALL):
        y = conv_rows(edges, bodies[f : f + PER_CALL + 2], gain_mid, w_mid, f, frames, own_rows, cols)
        y = y.reshape(n, chans, y.shape[1])
        parts = []
        for s in range(n):
            part = lax.dynamic_index_in_dim(y, me ^ s, 0, False)
            parts.append(part if s == 0 else lax.ppermute(part, "chan", [(i, i ^ s) for i in range(n)]))
        outs.append(parts)
    return finish(outs, features, own(bias_mid), me)


def solution(mesh):
    placed = (
        P("chan", ("grp", "tm"), None, None),
        P(),
        P(),
        P(None, None, None, "chan", None),
        P(),
        P(),
        P(None, None, None, "chan", None),
    )
    return jax.shard_map(
        per_device,
        mesh=mesh,
        in_specs=placed,
        out_specs=P("chan", ("grp", "tm"), None, None),
        check_vma=False,
    )
```
